32 devices in a mesh: row: 8 (over z, y), col: 4 (over x, core).
Axes of the slice: x: 2, y: 2, z: 4, core: 2. Of those that a mesh axis runs over, the one named last changes fastest.
Arguments:
- orbitals: float32 [2048, 28672], P(('row', 'col')), may hold values from -0.03125 to 0.03125
- applied: float32 [2048, 28672], P(('row', 'col')), may hold values from -6 to 6
Outputs:
- hamiltonian: float32 [2048, 2048], P('col', 'row')
- intersection: float32 [2048, 2048], P('col', 'row')
The draws below stay inside these ranges and needn't reach their ends.
All inputs are finite; a program needn't handle non-finite values.
Results may differ from the reference program's by a relative error of at most 0.000098.
Values sent between devices are 32-bit elements; how exact they have to be, the bound alone decides.
A program may use at most 192 MiB of HBM per device.

```python
import jax
import jax.numpy as jnp
from jax import lax

NORB = 2048
NCOEF = 28672


def strengthened(values, stream_key, source, target, shards_of, factor):
    def block_of(dim):
        return (jnp.arange(values.shape[dim]) // (values.shape[dim] // shards_of)).reshape((-1,) + (1,) * (values.ndim - 1 - dim))

    near = jax.random.permutation(stream_key, shards_of)[block_of(target)]
    other_side = (block_of(target) + shards_of // 2) % shards_of
    return jnp.where((block_of(source) == near) | (block_of(source) == other_side), factor * values, values)


def block_scale(rng, extent, pieces, smallest, largest):
    gain, own = 1.0, jax.random.fold_in(rng, 6)
    for position, parts in pieces:
        steps = jnp.exp(jax.random.uniform(jax.random.fold_in(own, position), (parts,), jnp.float32, smallest / len(pieces), largest / len(pieces)))
        gain = gain * jnp.repeat(steps, extent[position] // parts).reshape([-1 if axis == position else 1 for axis in range(len(extent))])
    return gain


def noise(key, dims, spread, bound, split=(), dtype=jnp.bfloat16):
    level = block_scale(key, dims, split, -0.22, 0.18) if split else 1.0
    values = jax.random.normal(key, dims, jnp.float32) * spread * level
    return jnp.minimum(jnp.maximum(values, -bound), bound).astype(dtype)


def noise_with(stream_key, extent, deviation, most, pieces, heavy, dtype=jnp.bfloat16):
    drawn = deviation * jax.random.normal(stream_key, extent, jnp.float32)
    if pieces:
        drawn = drawn * block_scale(stream_key, extent, pieces, -0.22, 0.18)
    return jnp.clip(strengthened(drawn, jax.random.fold_in(stream_key, 3), *heavy), -most, most).astype(dtype)


def setup_inputs(seed: int = 0) -> dict:
    key_of = jax.random.split(jax.random.key(seed), 3)
    return {
        "orbitals": noise(key_of[0], (NORB, NCOEF), NCOEF ** -0.5, 0.03125, ((0, 32),), jnp.float32),
        "applied": noise_with(key_of[1], (NORB, NCOEF), 1.0, 6.0, ((0, 32),), (1, 0, 32, 2.75), jnp.float32),
    }


def reference(orbitals, applied):
    hamiltonian = jnp.dot(orbitals, applied.T, precision=lax.Precision.HIGHEST, preferred_element_type=jnp.float32)
    intersection = jnp.dot(orbitals, orbitals.T, precision=lax.Precision.HIGHEST, preferred_element_type=jnp.float32)
    return hamiltonian, intersection
```

```python
import jax
import jax.numpy as jnp
from jax import lax
from jax.sharding import PartitionSpec as P


def product(left, right):
    return lax.dot_general(
        left,
        right,
        (((1,), (1,)), ((), ())),
        precision=lax.Precision.HIGH,
        preferred_element_type=jnp.float32,
    )


def shards(orbitals, applied):
    mine_orb, mine_app = (
        lax.all_to_all(orbitals, "col", split_axis=1, concat_axis=0, tiled=True),
        lax.all_to_all(applied, "col", split_axis=1, concat_axis=0, tiled=True),
    )
    every_orb = lax.all_gather(mine_orb, "row", axis=0, tiled=True)
    ham_part = product(every_orb, mine_app)
    ovl_part = product(every_orb, mine_orb)
    hamiltonian, intersection = (
        lax.psum_scatter(ham_part, "col", scatter_dimension=0, tiled=True),
        lax.psum_scatter(ovl_part, "col", scatter_dimension=0, tiled=True),
    )
    return (hamiltonian, intersection)


def solution(mesh):
    placed = (P(("row", "col"), None), P(("row", "col"), None))
    return jax.shard_map(
        shards,
        mesh=mesh,
        in_specs=placed,
        out_specs=(P("col", "row"), P("col", "row")),
        check_vma=False,
    )
```
